32 devices in a mesh: row: 4 (over y, x), col: 8 (over z, core).
Axes of the slice: x: 2, y: 2, z: 4, core: 2. Of those that a mesh axis runs over, the one named last changes fastest.
Arguments:
- tokens: bfloat16 [4096, 3584], P(('row', 'col')), may hold values from -6 to 6
- expert_ids: int32 [4096, 4], P(('row', 'col')), may hold values from 0 to 31, all different within a row; in each aligned block of 128 rows (0 to 127, 128 to 255, ...) at most 20 rows name the same one
- combine_weights: float32 [4096, 4], P(('row', 'col')), may hold values from 0.1 to 1
- expert_gate: bfloat16 [32, 3584, 1024], P(('row', 'col')), may hold values from -0.09375 to 0.09375
- expert_up: bfloat16 [32, 3584, 1024], P(('row', 'col')), may hold values from -0.09375 to 0.09375
- expert_down: bfloat16 [32, 1024, 3584], P(('row', 'col')), may hold values from -0.1875 to 0.1875
- shared_gate: bfloat16 [3584, 1024], P(None, 'row'), may hold values from -0.09375 to 0.09375
- shared_up: bfloat16 [3584, 1024], P(None, 'row'), may hold values from -0.09375 to 0.09375
- shared_down: bfloat16 [1024, 3584], P('row'), may hold values from -0.1875 to 0.1875
Outputs:
- mixed: bfloat16 [4096, 3584], P(('row', 'col'))
The draws below stay inside these ranges and needn't reach their ends.
Inputs may be any that keep to these rules, and one draw needn't show every extreme that they name: `expert_ids`: each row names 4 different experts. Among the 128 rows of one device no expert is named by more than 20 rows, and in every draw some expert is named by exactly 20 rows of some device.
All inputs are finite; a program needn't handle non-finite values.
Results may differ from the reference program's by a relative error of at most 0.0055.
Values may be sent and summed in bfloat16 or wider, within the bound.
No kernel may reach another device: no remote copies, remote signals or barrier semaphores. Data moves between devices by JAX's collectives and lax.ppermute only.
A program may use at most 128 MiB of HBM per device.

```python
import math
import jax
import jax.numpy as jnp
import numpy as np
from jax import lax

D = 3584
FF = 1024
SFF = 1024
TOP = 4
TOK_DEV = 128
EXPERTS = 32
TOKENS = 4096
CAP = 20
N_ROW = 4
N_COL = 8


def shard_levels(own_key, extent, split, smallest, high):
    factor_of = 1.0
    for position, blocks in split:
        heights = jax.random.uniform(jax.random.fold_in(jax.random.fold_in(own_key, 6), position), (blocks,), jnp.float32, smallest / len(split), high / len(split))
        factor_of = factor_of * jnp.repeat(jnp.exp(heights), extent[position] // blocks).reshape((-1,) + (1,) * (len(extent) - 1 - position))
    return factor_of


def routed_block(rng, own, number, rows, amount, top, most, slope):
    ranking = jax.random.permutation(rng, amount)
    heavy_load, ordinary = portions_of(amount, rows * top, most, slope, True), portions_of(amount, rows * top, most, slope, False)
    places = jnp.arange(amount)

    def named(lengths, rotation):
        used = int((lengths > 0).sum())
        fixed = max(1, used // 4)
        passed = fixed + (places - fixed + rotation * (used - fixed)) % max(1, amount - fixed)
        return jnp.zeros((amount,), jnp.int32).at[ranking[jnp.where(places < fixed, places, passed)]].set(jnp.asarray(lengths, jnp.int32))

    lengths = jnp.where(number % 4 == 0, named(heavy_load, number // 4), named(ordinary, number - number // 4 - 1))
    mixed = jax.random.permutation(jax.random.fold_in(own, 3), amount)
    source_of, sink = mixed[0:amount // 2 * 2:2], mixed[1:amount // 2 * 2:2]
    room = jnp.minimum(lengths[source_of] - 1, most - lengths[sink]) // 2
    room = jnp.where((source_of == ranking[0]) | (sink == ranking[0]) | (lengths[sink] == 0), 0, jnp.maximum(room, 0))
    passed = jax.random.randint(jax.random.fold_in(own, 4), (amount // 2,), 0, 1 << 20) % (room + 1)
    lengths = lengths.at[source_of].add(-passed).at[sink].add(passed)
    members = jnp.searchsorted(jnp.cumsum(lengths), jnp.arange(rows * top), side="right").astype(jnp.int32)
    listing = members.reshape(top, rows).T
    listing = listing[jax.random.permutation(jax.random.fold_in(own, 1), rows)]
    rotation = jax.random.randint(jax.random.fold_in(own, 2), (rows, 1), 0, top)
    return jnp.take_along_axis(listing, (jnp.arange(top)[None, :] + rotation) % top, axis=1)


def portions_of(number_of, total, bound, lean, full):
    portions = [(1 << 20) // math.isqrt(grade ** lean) + 1 for grade in range(1, number_of + 1)]
    largest = bound if full else min(bound, max(-(-total // number_of), total * portions[0] // sum(portions)))
    least = 1 if total - largest >= number_of - 1 else 0
    holding, spare = [largest] + [least] * (number_of - 1), total - largest - least * (number_of - 1)
    while spare > 0:
        free = [i for i in range(1, number_of) if holding[i] < largest] or [i for i in range(1, number_of) if holding[i] < bound]
        whole, budget = sum([portions[i] for i in free]), spare
        for i in free:
            addition = min(bound - holding[i], max(1, budget * portions[i] // whole), spare)
            holding[i] = holding[i] + addition
            spare = spare - addition
    return np.array(holding)


def noise(stream_key, dims, deviation, bound, cuts=(), kind=jnp.bfloat16):
    drawn = jax.random.normal(stream_key, dims, jnp.float32) * deviation
    if len(cuts) > 0:
        drawn = shard_levels(stream_key, dims, cuts, -0.22, 0.18) * drawn
    return jnp.clip(drawn, min=-bound, max=bound).astype(kind)


def setup_inputs(seed: int = 0) -> dict:
    streams_of = jax.random.split(jax.random.key(seed), 10)
    tokens = noise(streams_of[0], (TOKENS, D), 1.0, 6.0, ((0, 32),))
    expert_ids_keys = jax.random.split(jax.random.fold_in(streams_of[1], 1), TOKENS // TOK_DEV)
    expert_ids_turns = jax.random.permutation(jax.random.fold_in(streams_of[1], 3), TOKENS // TOK_DEV)
    expert_ids = jax.vmap(lambda own, number: routed_block(jax.random.fold_in(streams_of[1], 2), own, number, TOK_DEV, EXPERTS, TOP, CAP, 2))(expert_ids_keys, expert_ids_turns).reshape((TOKENS, TOP))
    combine_weights = jnp.clip(0.1 + 0.9 * jax.random.uniform(streams_of[2], (TOKENS, TOP), jnp.float32) ** shard_levels(streams_of[2], (TOKENS, TOP), ((0, 32),), -0.2, 0.2), 0.1, 1.0)
    expert_gate = noise(streams_of[3], (EXPERTS, D, FF), D ** -0.5, 0.09375, ((0, 32),))
    expert_up = noise(streams_of[4], (EXPERTS, D, FF), D ** -0.5, 0.09375, ((0, 32),))
    expert_down = noise(streams_of[5], (EXPERTS, FF, D), FF ** -0.5, 0.1875, ((0, 32),))
    shared_gate = noise(streams_of[6], (D, SFF), D ** -0.5, 0.09375, ((1, 4),))
    shared_up = noise(streams_of[7], (D, SFF), D ** -0.5, 0.09375, ((1, 4),))
    shared_down = noise(streams_of[8], (SFF, D), SFF ** -0.5, 0.1875, ((0, 4),))
    return dict(tokens=tokens, expert_ids=expert_ids, combine_weights=combine_weights, expert_gate=expert_gate, expert_up=expert_up, expert_down=expert_down, shared_gate=shared_gate, shared_up=shared_up, shared_down=shared_down)


def expert_mlp(token_rows, gate_w, up_w, down_w):
    gate_proj = jnp.dot(token_rows, gate_w, preferred_element_type=jnp.float32)
    up_proj = jnp.dot(token_rows, up_w, preferred_element_type=jnp.float32)
    hidden = (jax.nn.silu(gate_proj) * up_proj).astype(jnp.bfloat16)
    return jnp.dot(hidden, down_w, preferred_element_type=jnp.float32).astype(jnp.bfloat16)


def place_slots(choices, experts, capacity):
    flat_ids = choices.reshape(-1).astype(jnp.int32)
    onehot = (flat_ids[:, None] == jnp.arange(experts, dtype=jnp.int32)[None, :]).astype(jnp.int32)
    running = jnp.cumsum(onehot, axis=0)
    slot_rank = jnp.sum(onehot * running, axis=1) - 1
    return flat_ids * capacity + slot_rank


def reference(tokens, expert_ids, combine_weights, expert_gate, expert_up, expert_down, shared_gate, shared_up, shared_down):
    devices = N_ROW * N_COL
    experts = devices
    per_device = expert_ids.reshape(devices, TOK_DEV, TOP)
    targets = jax.vmap(lambda chosen: place_slots(chosen, experts, CAP))(per_device)
    owner_row = jnp.arange(TOK_DEV * TOP, dtype=jnp.int32) // TOP

    def make_table(target):
        return jnp.full((experts * CAP,), -1, jnp.int32).at[target].set(owner_row)

    tables = jax.vmap(make_table)(targets)
    filled = tables >= 0
    global_rows = jnp.maximum(tables, 0) + (jnp.arange(devices, dtype=jnp.int32) * TOK_DEV)[:, None]

    def one_expert(inputs):
        number, gate_w, up_w, down_w = inputs
        row_index = lax.dynamic_slice_in_dim(global_rows, number * CAP, CAP, 1).reshape(-1)
        live = lax.dynamic_slice_in_dim(filled, number * CAP, CAP, 1).reshape(-1)
        token_rows = jnp.where(live[:, None], tokens[row_index], jnp.zeros((), jnp.bfloat16))
        return expert_mlp(token_rows, gate_w, up_w, down_w)

    results = lax.map(one_expert, (jnp.arange(experts, dtype=jnp.int32), expert_gate, expert_up, expert_down))
    flat_results = results.reshape(-1, D)

    def combine_device(inputs):
        source, target, weights = inputs
        expert_of = target // CAP
        slot_of = target % CAP
        index = expert_of * (devices * CAP) + source * CAP + slot_of
        picked = flat_results[index].reshape(TOK_DEV, TOP, D)
        return jnp.sum(picked.astype(jnp.float32) * weights[:, :, None], axis=1)

    routed = lax.map(combine_device, (jnp.arange(devices, dtype=jnp.int32), targets, combine_weights.reshape(devices, TOK_DEV, TOP)))
    routed = routed.reshape(TOKENS, D)
    gate_proj = jnp.dot(tokens, shared_gate, preferred_element_type=jnp.float32)
    up_proj = jnp.dot(tokens, shared_up, preferred_element_type=jnp.float32)
    shared_hidden = (jax.nn.silu(gate_proj) * up_proj).astype(jnp.bfloat16)
    shared = jnp.dot(shared_hidden, shared_down, preferred_element_type=jnp.float32)
    return (routed + shared).astype(jnp.bfloat16)
```

```python
import jax
import jax.numpy as jnp
from jax import lax
from jax.sharding import Mesh, PartitionSpec as P


CHUNKS = 4
SWAP = [(0, 1), (1, 0)]


def dot32(a, b):
    return jnp.dot(a, b, preferred_element_type=jnp.float32)


def routing_tables(ids_t, weights_t, first_expert, experts, block, capacity):
    total = ids_t.shape[1]
    hits = ids_t[None, :, :] == first_expert[:, :, None]
    member = jnp.any(hits, axis=1)
    weight = jnp.sum(jnp.where(hits, weights_t[None, :, :], 0.0), axis=1)
    at = jnp.arange(total, dtype=jnp.int32)
    earlier = (at[:, None] < at[None, :]) & (at[:, None] // block == at[None, :] // block)
    rank = dot32(member.astype(jnp.bfloat16), earlier.astype(jnp.bfloat16)).astype(jnp.int32)
    slot = jnp.where(member, rank + (at // block * capacity)[None, :], -1)
    slots = total // block * capacity
    place = slot[:, None, :] == jnp.arange(slots, dtype=jnp.int32)[None, :, None]
    place = place.reshape(experts * slots, total)
    weighted = jnp.where(place, jnp.repeat(weight, slots, axis=0), 0.0)
    high = lax.reduce_precision(weighted, 8, 7)
    low = weighted - high
    combine = jnp.concatenate([high, low], axis=1).astype(jnp.bfloat16).T
    return place.astype(jnp.bfloat16), combine


def make_per_device(rows, halves, inner):
    group = rows * inner
    experts_all = group * halves
    bits = [1 << b for b in range(rows.bit_length() - 1)]

    def flip(value, bit):
        return lax.ppermute(value, "row", [(i, i ^ bit) for i in range(rows)])

    def per_device(tokens, expert_ids, combine_weights, expert_gate, expert_up, expert_down,
                   shared_gate, shared_up, shared_down):
        block, width = tokens.shape
        choices = expert_ids.shape[1]
        capacity = max(2, 5 * block * choices // (4 * experts_all))
        step = width // CHUNKS
        cuts = [slice(c * step, (c + 1) * step) for c in range(CHUNKS)]

        here = [tokens[:, cut] for cut in cuts]
        notes = jnp.concatenate([expert_ids.astype(jnp.float32), combine_weights], axis=1)
        notes = jnp.concatenate([notes, lax.ppermute(notes, "half", SWAP)], axis=0).T
        there = [lax.ppermute(part, "half", SWAP) for part in here]

        ids_t = notes[:choices].astype(jnp.int32)
        peer = jnp.arange(group, dtype=jnp.int32)
        number = (peer // inner * halves + lax.axis_index("half")) * inner + peer % inner
        place, combine = routing_tables(ids_t, notes[choices:], number[:, None], group, block, capacity)
        slots = halves * capacity

        gate = up = None
        for c, cut in enumerate(cuts):
            both = jnp.concatenate([here[c], there[c]], axis=0)
            outgoing = dot32(place, both).astype(jnp.bfloat16).reshape(group, slots, step)
            arrived = lax.all_to_all(outgoing, ("row", "inner"), 0, 0, tiled=True).reshape(group * slots, step)
            gate_part = dot32(arrived, expert_gate[0, cut])
            up_part = dot32(arrived, expert_up[0, cut])
            gate = gate_part if gate is None else gate + gate_part
            up = up_part if up is None else up + up_part
        hidden = (jax.nn.silu(gate) * up).astype(jnp.bfloat16)

        mid = width // 2
        gathered = []
        for cut, order in ((slice(0, mid), bits), (slice(mid, width), bits[::-1])):
            held = tokens[:, cut][None]
            for bit in order:
                held = jnp.concatenate([held, flip(held, bit)], axis=0)
            at = [0]
            for bit in order:
                at = at + [a ^ bit for a in at]
            gathered.append(jnp.concatenate([held[at.index(i)] for i in range(rows)], axis=0))
        row_tokens = jnp.concatenate(gathered, axis=1)
        shared_hidden = (jax.nn.silu(dot32(row_tokens, shared_gate)) * dot32(row_tokens, shared_up)).astype(jnp.bfloat16)
        shared = []
        for cut, order in ((slice(0, mid), bits), (slice(mid, width), bits[::-1])):
            sums = dot32(shared_hidden, shared_down[:, cut]).reshape(rows, block, mid)
            held = {i: sums[i] for i in range(rows)}
            for bit in order[::-1]:
                keep = [i for i in held if not i & bit]
                away = jnp.stack([held[i ^ bit] for i in keep]).astype(jnp.bfloat16)
                back = flip(away, bit)
                held = {i: held[i] + back[n] for n, i in enumerate(keep)}
            shared.append(held[0])
        shared = jnp.concatenate(shared, axis=1)

        mixed = []
        for c, cut in enumerate(cuts):
            results = dot32(hidden, expert_down[0, :, cut]).astype(jnp.bfloat16).reshape(group, slots, step)
            returned = lax.all_to_all(results, ("row", "inner"), 0, 0, tiled=True).reshape(group * slots, step)
            sums = dot32(combine, returned).reshape(2, halves * block, step)
            sums = sums[0] + sums[1]
            other = lax.ppermute(sums[block:].astype(jnp.bfloat16), "half", SWAP)
            mixed.append((sums[:block] + other + shared[:, cut]).astype(jnp.bfloat16))
        return jnp.concatenate(mixed, axis=1)

    return per_device


def solution(mesh):
    rows, cols = mesh.shape["row"], mesh.shape["col"]
    halves = 2
    split = Mesh(mesh.devices.reshape(rows, halves, cols // halves), ("row", "half", "inner"))
    everywhere = ("row", "half", "inner")
    return jax.shard_map(
        make_per_device(rows, halves, cols // halves),
        mesh=split,
        in_specs=(
            P(everywhere, None),
            P(everywhere, None),
            P(everywhere, None),
            P(everywhere, None, None),
            P(everywhere, None, None),
            P(everywhere, None, None),
            P(None, "row"),
            P(None, "row"),
            P("row", None),
        ),
        out_specs=P(everywhere, None),
        check_vma=False,
    )
```
